32 devices in a mesh: rows: 8 (over y, x, core), snaps: 4 (over z).
Axes of the slice: x: 2, y: 2, z: 4, core: 2. Of those that a mesh axis runs over, the one named last changes fastest.
Arguments:
- snapshots: float32 [2048, 3072], P('rows', 'snaps'), may hold values from -6 to 6
Outputs:
- updated: float32 [2048, 3072], P('rows', 'snaps')
- factor_rows: float32 [1152, 3072], P(None, 'snaps')
The draws below stay inside these ranges and needn't reach their ends.
All inputs are finite; a program needn't handle non-finite values.
Results may differ from the reference program's by a relative error of at most 0.00013.
Values sent between devices are 32-bit elements; how exact they have to be, the bound alone decides.
A program may use at most 64 MiB of HBM per device.

```python
import jax
import jax.numpy as jnp
from jax import lax

PANEL = 384
PANELS = 3
NROWS = 2048
NCOLS = 3072
N_SNAPS = 4


def level_of(own_key, shape, shards, low, high):
    factor_of = 1.0
    for axis_at, blocks in shards:
        draws = jax.random.uniform(jax.random.fold_in(jax.random.fold_in(own_key, 6), axis_at), (blocks,), jnp.float32, low / len(shards), high / len(shards))
        factor_of = factor_of * jnp.repeat(jnp.exp(draws), shape[axis_at] // blocks).reshape((-1,) + (1,) * (len(shape) - 1 - axis_at))
    return factor_of


def normal_values(key, extent, width, limit, pieces=(), kind=jnp.bfloat16):
    entries = width * jax.random.normal(key, extent, jnp.float32)
    if pieces:
        entries = entries * level_of(key, extent, pieces, -0.22, 0.18)
    return jnp.clip(entries, -limit, limit).astype(kind)


def setup_inputs(seed: int = 0) -> dict:
    keys = jax.random.split(jax.random.key(seed), 2)
    snapshots = normal_values(keys[0], (NROWS, NCOLS), 1.0, 6.0, ((0, 8), (1, 4)), jnp.float32)
    return {"snapshots": snapshots}


def mult(left, right):
    return jnp.dot(left.astype(jnp.float32), right.astype(jnp.float32), precision=lax.Precision.HIGHEST, preferred_element_type=jnp.float32)

def reference(snapshots):
    row_count, col_count = snapshots.shape
    panel_width = PANEL
    block_count = col_count // panel_width
    per_device = block_count // N_SNAPS
    block_ids = jnp.arange(block_count, dtype=jnp.int32)
    sequence = block_ids % per_device * N_SNAPS + block_ids // per_device
    turn_cols = jnp.repeat(sequence, panel_width)
    root_rows = jnp.sqrt(jnp.float32(row_count))
    identity = jnp.eye(panel_width, dtype=jnp.float32)
    working = snapshots
    coeff_rows = []
    for section in range(PANELS):
        owner_index = section % N_SNAPS
        slot_index = section // N_SNAPS
        offset = (owner_index * per_device + slot_index) * panel_width
        panel_now = working[:, offset:offset + panel_width]
        gram_matrix = mult(panel_now.T, panel_now)
        factor = jnp.linalg.cholesky(gram_matrix)
        inverse = lax.linalg.triangular_solve(factor, identity, left_side=True, lower=True)
        orthobasis = mult(panel_now, inverse.T)
        coeffs = mult(orthobasis.T, working)
        applied = jnp.where((turn_cols > section)[None, :], coeffs, jnp.float32(0.0))
        working = working - mult(orthobasis, applied)
        working = working.at[:, offset:offset + panel_width].set(orthobasis * root_rows)
        diagonal = jnp.where((turn_cols == section)[None, :], jnp.tile(factor.T, (1, block_count)), jnp.float32(0.0))
        coeff_rows.append((applied + diagonal) / root_rows)
    return (working, jnp.concatenate(coeff_rows, axis=0))
```

```python
import functools

import jax
import jax.numpy as jnp
from jax import lax
from jax.experimental import pallas as pl
from jax.experimental.pallas import tpu as pltpu
from jax.sharding import PartitionSpec as P

PANEL = 384
PANELS = 3
F32 = jnp.float32
BF16 = jnp.bfloat16


def dims(ta, tb):
    return (((0 if ta else 1,), (1 if tb else 0,)), ((), ()))


def dot6(a, b, ta=False, tb=False):
    return lax.dot_general(
        a, b, dims(ta, tb), precision=lax.Precision.HIGHEST, preferred_element_type=F32
    )


def dot1(a, b, ta=False, tb=False):
    return lax.dot_general(
        a.astype(BF16), b.astype(BF16), dims(ta, tb), preferred_element_type=F32
    )


def dot3(a, b, ta=False, tb=False):
    a_hi, b_hi = a.astype(BF16), b.astype(BF16)
    a_lo = (a - a_hi.astype(F32)).astype(BF16)
    b_lo = (b - b_hi.astype(F32)).astype(BF16)
    d = dims(ta, tb)
    return (
        lax.dot_general(a_hi, b_lo, d, preferred_element_type=F32)
        + lax.dot_general(a_lo, b_hi, d, preferred_element_type=F32)
        + lax.dot_general(a_hi, b_hi, d, preferred_element_type=F32)
    )


def grid_ids(n):
    return (
        lax.broadcasted_iota(jnp.int32, (n, n), 0),
        lax.broadcasted_iota(jnp.int32, (n, n), 1),
    )


def direct_inverse(x_ref, a_ref):
    n = a_ref.shape[0]
    row_ids, col_ids = grid_ids(n)
    x_ref[...] = jnp.where(row_ids == col_ids, F32(1), F32(0))

    @pl.loop(0, n)
    def _(j):
        a = a_ref[...]
        a_row = jnp.sum(jnp.where(row_ids == j, a, F32(0)), axis=0, keepdims=True)
        x = x_ref[...]
        x_row = jnp.sum(jnp.where(row_ids == j, x, F32(0)), axis=0, keepdims=True)
        a_col = jnp.sum(jnp.where(col_ids == j, a, F32(0)), axis=1, keepdims=True)
        pivot = jnp.sum(jnp.where(col_ids[:1] == j, a_row, F32(0)), axis=1, keepdims=True)
        ratio = jnp.where(row_ids[:, :1] > j, a_col / pivot, F32(0))
        a_ref[...] = a - ratio * a_row
        x_ref[...] = jnp.where(row_ids == j, x / jnp.sqrt(pivot), x - ratio * x_row)


def newton_inverse(x_ref, a_ref):
    n = a_ref.shape[0]
    row_ids, col_ids = grid_ids(n)
    on_diag = row_ids == col_ids
    a = a_ref[...]
    diag = jnp.sum(jnp.where(on_diag, a, F32(0)), axis=1, keepdims=True)
    x_ref[...] = jnp.where(on_diag, lax.rsqrt(diag), F32(0))

    def step(dot):
        x = x_ref[...]
        err = dot(dot(x, a_ref[...]), x, tb=True) - jnp.where(on_diag, F32(1), F32(0))
        half = jnp.where(row_ids > col_ids, err, jnp.where(on_diag, F32(0.5) * err, F32(0)))
        x_ref[...] = x - dot(half, x)
        return jnp.sum(err * err)

    def rough(state):
        count, size = state
        return count + 1, step(dot1)

    def fine(state):
        count, size = state
        return count + 1, step(dot6)

    count, size = lax.while_loop(
        lambda s: (s[0] < 12) & (s[1] > F32(0.5)), rough, (jnp.int32(0), F32(1e9))
    )
    count, size = lax.while_loop(
        lambda s: (s[0] < 24) & (s[1] > F32(1e-6)), fine, (count, F32(1e9))
    )

    @pl.when(jnp.logical_not(size <= F32(1e-6)))
    def _():
        direct_inverse(x_ref, a_ref)


def factor_kernel(root_rows, p_ref, w_ref, m_ref, g_ref, out_ref, fac_ref, q_ref, u_ref, c_ref, t_ref, x_ref):
    snap = lax.axis_index("snaps")
    n = PANEL
    row_ids, col_ids = grid_ids(n)
    width = w_ref.shape[1]
    chunks = [(c, n) for c in range(0, width, n)]

    def blk(k):
        return slice(k * n, (k + 1) * n)

    for k in range(PANELS):
        acc = m_ref[blk(k), blk(k)]
        for j in range(k):
            acc = acc - dot6(u_ref[blk(j), blk(k)], u_ref[blk(j), blk(k)], ta=True)
        t_ref[...] = acc
        newton_inverse(x_ref, t_ref)
        x = x_ref[...]
        for i in range(k + 1, PANELS):
            acc = m_ref[blk(k), blk(i)]
            for j in range(k):
                acc = acc - dot6(u_ref[blk(j), blk(k)], u_ref[blk(j), blk(i)], ta=True)
            u_ref[blk(k), blk(i)] = dot6(x, acc)
        for low, size in chunks:
            cols = slice(low, low + size)
            acc = g_ref[blk(k), cols]
            for j in range(k):
                acc = acc - dot3(u_ref[blk(j), blk(k)], c_ref[blk(j), cols], ta=True)
            coeffs = dot3(x, acc)
            if low == 0:
                keep = (snap > k) | ((snap == k) & (row_ids <= col_ids))
                coeffs = jnp.where(keep, coeffs, F32(0))
            c_ref[blk(k), cols] = coeffs
            fac_ref[blk(k), cols] = coeffs / root_rows
        rest = p_ref[:, blk(k)]
        for j in range(k):
            rest = rest - dot3(q_ref[:, blk(j)], u_ref[blk(j), blk(k)])
        q_ref[:, blk(k)] = dot3(rest, x, tb=True)

    for low, size in chunks:
        cols = slice(low, low + size)
        acc = w_ref[:, cols]
        for k in range(PANELS):
            acc = acc - dot3(q_ref[:, blk(k)], c_ref[blk(k), cols])
        out_ref[:, cols] = acc
    for k in range(PANELS):

        @pl.when(snap == k)
        def _():
            out_ref[:, :n] = q_ref[:, blk(k)] * root_rows


def shards(snapshots):
    rows_dev, cols_dev = snapshots.shape
    row_count = rows_dev * lax.axis_size("rows")
    root_rows = float(row_count) ** 0.5
    total = PANEL * PANELS
    panels = lax.all_gather(snapshots[:, :PANEL], "snaps", axis=1, tiled=True)[:, :total]
    gram, cross = lax.psum(
        (dot6(panels, panels, ta=True), dot6(panels, snapshots, ta=True)), "rows"
    )
    vmem = pl.BlockSpec(memory_space=pltpu.VMEM)
    return pl.pallas_call(
        functools.partial(factor_kernel, root_rows),
        out_shape=(
            jax.ShapeDtypeStruct((rows_dev, cols_dev), F32),
            jax.ShapeDtypeStruct((total, cols_dev), F32),
        ),
        in_specs=[vmem] * 4,
        out_specs=(vmem, vmem),
        scratch_shapes=[
            pltpu.VMEM((rows_dev, total), F32),
            pltpu.VMEM((total, total), F32),
            pltpu.VMEM((total, cols_dev), F32),
            pltpu.VMEM((PANEL, PANEL), F32),
            pltpu.VMEM((PANEL, PANEL), F32),
        ],
        compiler_params=pltpu.CompilerParams(vmem_limit_bytes=56 * 2**20),
    )(panels, snapshots, gram, cross)


def solution(mesh):
    assert mesh.shape["snaps"] >= PANELS
    return jax.shard_map(
        shards,
        mesh=mesh,
        in_specs=(P("rows", "snaps"),),
        out_specs=(P("rows", "snaps"), P(None, "snaps")),
        check_vma=False,
    )
```

```python
import functools

import jax
import jax.numpy as jnp
from jax import lax
from jax.experimental import pallas as pl
from jax.experimental.pallas import tpu as pltpu
from jax.sharding import PartitionSpec as P

PANEL = 384
PANELS = 3
F32 = jnp.float32
BF16 = jnp.bfloat16


def dims(ta, tb):
    return (((0 if ta else 1,), (1 if tb else 0,)), ((), ()))


def dot6(a, b, ta=False, tb=False):
    return lax.dot_general(
        a, b, dims(ta, tb), precision=lax.Precision.HIGHEST, preferred_element_type=F32
    )


def dot1(a, b, ta=False, tb=False):
    return lax.dot_general(
        a.astype(BF16), b.astype(BF16), dims(ta, tb), preferred_element_type=F32
    )


def dot3(a, b, ta=False, tb=False):
    a_hi, b_hi = a.astype(BF16), b.astype(BF16)
    a_lo = (a - a_hi.astype(F32)).astype(BF16)
    b_lo = (b - b_hi.astype(F32)).astype(BF16)
    d = dims(ta, tb)
    return (
        lax.dot_general(a_hi, b_lo, d, preferred_element_type=F32)
        + lax.dot_general(a_lo, b_hi, d, preferred_element_type=F32)
        + lax.dot_general(a_hi, b_hi, d, preferred_element_type=F32)
    )


def grid_ids(n):
    return (
        lax.broadcasted_iota(jnp.int32, (n, n), 0),
        lax.broadcasted_iota(jnp.int32, (n, n), 1),
    )


def direct_inverse(x_ref, a_ref):
    n = a_ref.shape[0]
    row_ids, col_ids = grid_ids(n)
    x_ref[...] = jnp.where(row_ids == col_ids, F32(1), F32(0))

    @pl.loop(0, n)
    def _(j):
        a = a_ref[...]
        a_row = jnp.sum(jnp.where(row_ids == j, a, F32(0)), axis=0, keepdims=True)
        x = x_ref[...]
        x_row = jnp.sum(jnp.where(row_ids == j, x, F32(0)), axis=0, keepdims=True)
        a_col = jnp.sum(jnp.where(col_ids == j, a, F32(0)), axis=1, keepdims=True)
        pivot = jnp.sum(jnp.where(col_ids[:1] == j, a_row, F32(0)), axis=1, keepdims=True)
        ratio = jnp.where(row_ids[:, :1] > j, a_col / pivot, F32(0))
        a_ref[...] = a - ratio * a_row
        x_ref[...] = jnp.where(row_ids == j, x / jnp.sqrt(pivot), x - ratio * x_row)


def newton_inverse(x_ref, a_ref):
    n = a_ref.shape[0]
    row_ids, col_ids = grid_ids(n)
    on_diag = row_ids == col_ids
    a = a_ref[...]
    diag = jnp.sum(jnp.where(on_diag, a, F32(0)), axis=1, keepdims=True)
    x_ref[...] = jnp.where(on_diag, lax.rsqrt(diag), F32(0))

    def step(dot):
        x = x_ref[...]
        err = dot(dot(x, a_ref[...]), x, tb=True) - jnp.where(on_diag, F32(1), F32(0))
        half = jnp.where(row_ids > col_ids, err, jnp.where(on_diag, F32(0.5) * err, F32(0)))
        x_ref[...] = x - dot(half, x)
        return jnp.sum(err * err)

    def rough(state):
        count, size = state
        return count + 1, step(dot1)

    def fine(state):
        count, size = state
        return count + 1, step(dot6)

    count, size = lax.while_loop(
        lambda s: (s[0] < 12) & (s[1] > F32(0.5)), rough, (jnp.int32(0), F32(1e9))
    )
    count, size = lax.while_loop(
        lambda s: (s[0] < 24) & (s[1] > F32(1e-6)), fine, (count, F32(1e9))
    )

    @pl.when(jnp.logical_not(size <= F32(1e-6)))
    def _():
        direct_inverse(x_ref, a_ref)


def factor_kernel(root_rows, p_ref, w_ref, v0_ref, v1_ref, v2_ref, out_ref, fac_ref, q_ref, u_ref, c_ref, t_ref, x_ref):
    v_refs = (v0_ref, v1_ref, v2_ref)
    snap = lax.axis_index("snaps")
    n = PANEL
    row_ids, col_ids = grid_ids(n)
    width = w_ref.shape[1]
    chunks = [(c, n) for c in range(0, width, n)]

    def blk(k):
        return slice(k * n, (k + 1) * n)

    for k in range(PANELS):
        acc = v_refs[k][:, :n]
        for j in range(k):
            acc = acc - dot6(u_ref[blk(j), blk(k)], u_ref[blk(j), blk(k)], ta=True)
        t_ref[...] = acc
        newton_inverse(x_ref, t_ref)
        x = x_ref[...]
        for i in range(k + 1, PANELS):
            acc = v_refs[k][:, blk(i - k)]
            for j in range(k):
                acc = acc - dot6(u_ref[blk(j), blk(k)], u_ref[blk(j), blk(i)], ta=True)
            u_ref[blk(k), blk(i)] = dot6(x, acc)
        for low, size in chunks:
            cols = slice(low, low + size)
            shift = (PANELS - k) * n
            acc = v_refs[k][:, shift + low : shift + low + size]
            for j in range(k):
                acc = acc - dot3(u_ref[blk(j), blk(k)], c_ref[blk(j), cols], ta=True)
            coeffs = dot3(x, acc)
            if low == 0:
                keep = (snap > k) | ((snap == k) & (row_ids <= col_ids))
                coeffs = jnp.where(keep, coeffs, F32(0))
            c_ref[blk(k), cols] = coeffs
            fac_ref[blk(k), cols] = coeffs / root_rows
        rest = p_ref[:, blk(k)]
        for j in range(k):
            rest = rest - dot3(q_ref[:, blk(j)], u_ref[blk(j), blk(k)])
        q_ref[:, blk(k)] = dot3(rest, x, tb=True)

    for low, size in chunks:
        cols = slice(low, low + size)
        acc = w_ref[:, cols]
        for k in range(PANELS):
            acc = acc - dot3(q_ref[:, blk(k)], c_ref[blk(k), cols])
        out_ref[:, cols] = acc
    for k in range(PANELS):

        @pl.when(snap == k)
        def _():
            out_ref[:, :n] = q_ref[:, blk(k)] * root_rows


def bit_order(n_bits, half):
    return [0] + (list(range(1, n_bits)) if half == 0 else list(range(n_bits - 1, 0, -1)))


def reduce_kernel(n_rows, n_snaps, w_ref, p_ref, o0_ref, o1_ref, o2_ref, *scratch):
    v_refs, lands = scratch[:PANELS], scratch[PANELS:-5]
    z_send, z_recv, own_sem, send_sems, recv_sems = scratch[-5:]
    o_refs = (o0_ref, o1_ref, o2_ref)
    n = PANEL
    n_bits = n_rows.bit_length() - 1
    row = lax.axis_index("rows")
    snap = lax.axis_index("snaps")
    bits = [(row // 2**b) % 2 for b in range(n_bits)]
    mates = [row + (1 - 2 * bits[b]) * 2**b for b in range(n_bits)]
    up, down = lax.rem(snap + 1, n_snaps), lax.rem(snap + n_snaps - 1, n_snaps)

    barrier = pltpu.get_barrier_semaphore()
    for mate in mates:
        pl.semaphore_signal(barrier, inc=1, device_id={"rows": mate})
    for mate in (up, down):
        pl.semaphore_signal(barrier, inc=1, device_id={"snaps": mate})
    pl.semaphore_wait(barrier, n_bits + 2)

    def panel(k):
        return p_ref.at[:, k * n : (k + 1) * n]

    def relay(k, way):
        return pltpu.make_async_remote_copy(
            src_ref=panel(k),
            dst_ref=panel(k),
            send_sem=z_send.at[k, way],
            recv_sem=z_recv.at[k],
            device_id={"snaps": up if way else down},
        )

    def pass_on(k):
        @pl.when((snap >= k) & (snap < n_snaps - 1))
        def _():
            relay(k, 1).start()

        @pl.when((snap <= k) & (snap > 0))
        def _():
            relay(k, 0).start()

    for k in range(PANELS):

        @pl.when(snap == k)
        def _():
            own = pltpu.make_async_copy(w_ref.at[:, :n], panel(k), own_sem)
            own.start()
            own.wait()
            pass_on(k)

    order = list(range(PANELS - 1, -1, -1))

    def halves(k):
        width = v_refs[k].shape[1]
        split = (width // 256 + k // 2) * 128
        return ((0, split), (split, width - split))

    def spans(half):
        first, size, out = 0, n, []
        for b in bit_order(n_bits, half):
            size //= 2
            out.append((b, size, first + bits[b] * size, first + (1 - bits[b]) * size))
            first = first + bits[b] * size
        return out

    stages = [spans(0), spans(1)]

    def window(refs, k, half, first, size):
        low, width = halves(k)[half]
        return refs[k].at[pl.ds(pl.multiple_of(first, 8), size), low : low + width]

    def copy(k, half, step):
        down_step = step >= n_bits
        stage = 2 * n_bits - 1 - step if down_step else step
        b, size, kept, given = stages[half][stage]
        if down_step:
            src = dst = window(o_refs, k, half, kept, size)
        else:
            src = window(v_refs, k, half, given, size)
            dst = lands[(k * 2 + half) * n_bits + stage]
        return pltpu.make_async_remote_copy(
            src_ref=src,
            dst_ref=dst,
            send_sem=send_sems.at[k, half, step],
            recv_sem=recv_sems.at[k, half, step],
            device_id={"rows": mates[b]},
        )

    def finish(k, half, step):
        copy(k, half, step).wait_recv()
        if step < n_bits:
            b, size, kept, given = stages[half][step]
            view = window(v_refs, k, half, kept, size)
            into = view if step < n_bits - 1 else window(o_refs, k, half, kept, size)
            into[...] = view[...] + lands[(k * 2 + half) * n_bits + step][...]

    def compute(k):
        left = p_ref[:, k * n : (k + 1) * n]
        for i in range(k, PANELS):
            v_refs[k][:, (i - k) * n : (i - k + 1) * n] = dot6(
                left, p_ref[:, i * n : (i + 1) * n], ta=True
            )
        shift = (PANELS - k) * n
        for low in range(0, w_ref.shape[1], n):
            v_refs[k][:, shift + low : shift + low + n] = dot6(
                left, w_ref[:, low : low + n], ta=True
            )

    steps = 2 * n_bits
    for tick in range(steps + PANELS):
        for place, k in enumerate(order):
            step = tick - place
            if step == 0:

                @pl.when(snap != k)
                def _():
                    relay(k, 0).wait_recv()
                    pass_on(k)

                compute(k)
            for half in range(2):
                if 1 <= step <= steps:
                    finish(k, half, step - 1)
                if 0 <= step < steps:
                    copy(k, half, step).start()

    for k in range(PANELS):
        for half in range(2):
            for step in range(steps):
                copy(k, half, step).wait_send()

        @pl.when((snap >= k) & (snap < n_snaps - 1))
        def _():
            relay(k, 1).wait_send()

        @pl.when((snap <= k) & (snap > 0))
        def _():
            relay(k, 0).wait_send()


def reduced_by_copies(snapshots, n_rows, n_snaps):
    rows_dev, cols_dev = snapshots.shape
    n_bits = n_rows.bit_length() - 1
    widths = [(PANELS - k) * PANEL + cols_dev for k in range(PANELS)]
    lands = []
    for k, width in enumerate(widths):
        split = (width // 256 + k // 2) * 128
        for part in (split, width - split):
            lands += [pltpu.VMEM((PANEL >> (s + 1), part), F32) for s in range(n_bits)]
    vmem = pl.BlockSpec(memory_space=pltpu.VMEM)
    dma = pltpu.SemaphoreType.DMA
    return pl.pallas_call(
        functools.partial(reduce_kernel, n_rows, n_snaps),
        out_shape=[jax.ShapeDtypeStruct((rows_dev, PANELS * PANEL), F32)]
        + [jax.ShapeDtypeStruct((PANEL, width), F32) for width in widths],
        in_specs=[vmem],
        out_specs=[vmem] * (1 + PANELS),
        scratch_shapes=[pltpu.VMEM((PANEL, width), F32) for width in widths]
        + lands
        + [
            dma((PANELS, 2)),
            dma((PANELS,)),
            dma(()),
            dma((PANELS, 2, 2 * n_bits)),
            dma((PANELS, 2, 2 * n_bits)),
        ],
        compiler_params=pltpu.CompilerParams(
            collective_id=0, has_side_effects=True, vmem_limit_bytes=40 * 2**20
        ),
    )(snapshots)


def reduced_by_collectives(snapshots):
    total = PANEL * PANELS
    panels = lax.all_gather(snapshots[:, :PANEL], "snaps", axis=1, tiled=True)[:, :total]
    both = jnp.concatenate([panels, snapshots], axis=1)
    sums = lax.psum(
        [
            dot6(panels[:, k * PANEL : (k + 1) * PANEL], both[:, k * PANEL :], ta=True)
            for k in range(PANELS)
        ],
        "rows",
    )
    return [panels] + list(sums)


def shards(snapshots):
    rows_dev, cols_dev = snapshots.shape
    n_rows, n_snaps = lax.axis_size("rows"), lax.axis_size("snaps")
    root_rows = float(rows_dev * n_rows) ** 0.5
    total = PANEL * PANELS
    if n_rows & (n_rows - 1) == 0 and PANEL % (8 * n_rows) == 0:
        panels, *sums = reduced_by_copies(snapshots, n_rows, n_snaps)
    else:
        panels, *sums = reduced_by_collectives(snapshots)
    vmem = pl.BlockSpec(memory_space=pltpu.VMEM)
    return pl.pallas_call(
        functools.partial(factor_kernel, root_rows),
        out_shape=(
            jax.ShapeDtypeStruct((rows_dev, cols_dev), F32),
            jax.ShapeDtypeStruct((total, cols_dev), F32),
        ),
        in_specs=[vmem] * 5,
        out_specs=(vmem, vmem),
        scratch_shapes=[
            pltpu.VMEM((rows_dev, total), F32),
            pltpu.VMEM((total, total), F32),
            pltpu.VMEM((total, cols_dev), F32),
            pltpu.VMEM((PANEL, PANEL), F32),
            pltpu.VMEM((PANEL, PANEL), F32),
        ],
        compiler_params=pltpu.CompilerParams(vmem_limit_bytes=56 * 2**20),
    )(panels, snapshots, *sums)


def solution(mesh):
    assert mesh.shape["snaps"] >= PANELS
    return jax.shard_map(
        shards,
        mesh=mesh,
        in_specs=(P("rows", "snaps"),),
        out_specs=(P("rows", "snaps"), P(None, "snaps")),
        check_vma=False,
    )
```

```python
import functools

import jax
import jax.numpy as jnp
from jax import lax
from jax.experimental import pallas as pl
from jax.experimental.pallas import tpu as pltpu
from jax.sharding import PartitionSpec as P

PANEL = 384
PANELS = 3
F32 = jnp.float32
BF16 = jnp.bfloat16


def dims(ta, tb):
    return (((0 if ta else 1,), (1 if tb else 0,)), ((), ()))


def dot6(a, b, ta=False, tb=False):
    return lax.dot_general(
        a, b, dims(ta, tb), precision=lax.Precision.HIGHEST, preferred_element_type=F32
    )


def dot1(a, b, ta=False, tb=False):
    return lax.dot_general(
        a.astype(BF16), b.astype(BF16), dims(ta, tb), preferred_element_type=F32
    )


def dot3(a, b, ta=False, tb=False):
    a_hi, b_hi = a.astype(BF16), b.astype(BF16)
    a_lo = (a - a_hi.astype(F32)).astype(BF16)
    b_lo = (b - b_hi.astype(F32)).astype(BF16)
    d = dims(ta, tb)
    return (
        lax.dot_general(a_hi, b_lo, d, preferred_element_type=F32)
        + lax.dot_general(a_lo, b_hi, d, preferred_element_type=F32)
        + lax.dot_general(a_hi, b_hi, d, preferred_element_type=F32)
    )


def grid_ids(n):
    return (
        lax.broadcasted_iota(jnp.int32, (n, n), 0),
        lax.broadcasted_iota(jnp.int32, (n, n), 1),
    )


def direct_inverse(x_ref, a_ref):
    n = a_ref.shape[0]
    row_ids, col_ids = grid_ids(n)
    x_ref[...] = jnp.where(row_ids == col_ids, F32(1), F32(0))

    @pl.loop(0, n)
    def _(j):
        a = a_ref[...]
        a_row = jnp.sum(jnp.where(row_ids == j, a, F32(0)), axis=0, keepdims=True)
        x = x_ref[...]
        x_row = jnp.sum(jnp.where(row_ids == j, x, F32(0)), axis=0, keepdims=True)
        a_col = jnp.sum(jnp.where(col_ids == j, a, F32(0)), axis=1, keepdims=True)
        pivot = jnp.sum(jnp.where(col_ids[:1] == j, a_row, F32(0)), axis=1, keepdims=True)
        ratio = jnp.where(row_ids[:, :1] > j, a_col / pivot, F32(0))
        a_ref[...] = a - ratio * a_row
        x_ref[...] = jnp.where(row_ids == j, x / jnp.sqrt(pivot), x - ratio * x_row)


def newton_inverse(x_ref, a_ref):
    n = a_ref.shape[0]
    row_ids, col_ids = grid_ids(n)
    on_diag = row_ids == col_ids
    a = a_ref[...]
    diag = jnp.sum(jnp.where(on_diag, a, F32(0)), axis=1, keepdims=True)
    x_ref[...] = jnp.where(on_diag, lax.rsqrt(diag), F32(0))

    def step(dot, dot_half):
        x = x_ref[...]
        err = dot(dot(x, a_ref[...]), x, tb=True) - jnp.where(on_diag, F32(1), F32(0))
        half = jnp.where(row_ids > col_ids, err, jnp.where(on_diag, F32(0.5) * err, F32(0)))
        x_ref[...] = x - dot_half(half, x)
        return jnp.sum(err * err)

    def stage(state, dots, limit, count_limit):
        return lax.while_loop(
            lambda s: (s[0] < count_limit) & (s[1] > F32(limit)),
            lambda s: (s[0] + 1, step(*dots)),
            state,
        )

    count, size = stage((jnp.int32(0), F32(1e9)), (dot1, dot1), 0.3, 12)
    count, size = stage((count, F32(1e9)), (dot3, dot3), 1e-3, 20)
    count, size = stage((count, F32(1e9)), (dot6, dot3), 1e-6, 26)

    @pl.when(jnp.logical_not(size <= F32(1e-6)))
    def _():
        direct_inverse(x_ref, a_ref)


def factor_kernel(
    root_rows, p_hbm, w_hbm, v0_hbm, v1_hbm, v2_hbm, out_hbm, fac_hbm,
    p_ref, w_ref, v0_ref, v1_ref, v2_ref, out_ref, fac_ref,
    q_ref, u_ref, c_ref, t_ref, x_ref, in_sems, fac_sems, out_sems,
):
    v_refs = (v0_ref, v1_ref, v2_ref)
    snap = lax.axis_index("snaps")
    n = PANEL
    row_ids, col_ids = grid_ids(n)
    width = w_ref.shape[1]
    chunks = [(c, n) for c in range(0, width, n)]

    def blk(k):
        return slice(k * n, (k + 1) * n)

    loads = [
        pltpu.make_async_copy(v0_hbm.at[:, :n], v0_ref.at[:, :n], in_sems.at[0]),
        pltpu.make_async_copy(v0_hbm.at[:, n:], v0_ref.at[:, n:], in_sems.at[1]),
        pltpu.make_async_copy(p_hbm, p_ref, in_sems.at[2]),
        pltpu.make_async_copy(v1_hbm, v1_ref, in_sems.at[3]),
        pltpu.make_async_copy(v2_hbm, v2_ref, in_sems.at[4]),
        pltpu.make_async_copy(w_hbm, w_ref, in_sems.at[5]),
    ]
    for load in loads:
        load.start()
    loads[0].wait()
    stores = []

    for k in range(PANELS):
        acc = v_refs[k][:, :n]
        for j in range(k):
            acc = acc - dot6(u_ref[blk(j), blk(k)], u_ref[blk(j), blk(k)], ta=True)
        t_ref[...] = acc
        newton_inverse(x_ref, t_ref)
        if k == 0:
            for load in loads[1:]:
                load.wait()
        x = x_ref[...]
        for i in range(k + 1, PANELS):
            acc = v_refs[k][:, blk(i - k)]
            for j in range(k):
                acc = acc - dot3(u_ref[blk(j), blk(k)], u_ref[blk(j), blk(i)], ta=True)
            u_ref[blk(k), blk(i)] = dot3(x, acc)
        for low, size in chunks:
            cols = slice(low, low + size)
            shift = (PANELS - k) * n
            acc = v_refs[k][:, shift + low : shift + low + size]
            for j in range(k):
                acc = acc - dot3(u_ref[blk(j), blk(k)], c_ref[blk(j), cols], ta=True)
            coeffs = dot3(x, acc)
            if low == 0:
                keep = (snap > k) | ((snap == k) & (row_ids <= col_ids))
                coeffs = jnp.where(keep, coeffs, F32(0))
            c_ref[blk(k), cols] = coeffs
            fac_ref[blk(k), cols] = coeffs / root_rows
        stores.append(pltpu.make_async_copy(fac_ref.at[blk(k)], fac_hbm.at[blk(k)], fac_sems.at[k]))
        stores[-1].start()
        rest = p_ref[:, blk(k)]
        for j in range(k):
            rest = rest - dot3(q_ref[:, blk(j)], u_ref[blk(j), blk(k)])
        q_ref[:, blk(k)] = dot3(rest, x, tb=True)

    for at, (low, size) in enumerate(chunks):
        cols = slice(low, low + size)
        acc = w_ref[:, cols]
        for k in range(PANELS):
            acc = acc - dot3(q_ref[:, blk(k)], c_ref[blk(k), cols])
        if low == 0:
            for k in range(PANELS):
                acc = jnp.where(snap == k, q_ref[:, blk(k)] * root_rows, acc)
        out_ref[:, cols] = acc
        stores.append(pltpu.make_async_copy(out_ref.at[:, cols], out_hbm.at[:, cols], out_sems.at[at]))
        stores[-1].start()
    for store in stores:
        store.wait()


def bit_order(n_bits, half):
    return [0] + (list(range(1, n_bits)) if half == 0 else list(range(n_bits - 1, 0, -1)))


def reduce_kernel(n_rows, n_snaps, w_ref, p_ref, o0_ref, o1_ref, o2_ref, *scratch):
    v_refs, lands = scratch[:PANELS], scratch[PANELS:-5]
    z_send, z_recv, own_sem, send_sems, recv_sems = scratch[-5:]
    o_refs = (o0_ref, o1_ref, o2_ref)
    n = PANEL
    n_bits = n_rows.bit_length() - 1
    row = lax.axis_index("rows")
    snap = lax.axis_index("snaps")
    bits = [(row // 2**b) % 2 for b in range(n_bits)]
    mates = [row + (1 - 2 * bits[b]) * 2**b for b in range(n_bits)]
    up, down = lax.rem(snap + 1, n_snaps), lax.rem(snap + n_snaps - 1, n_snaps)

    barrier = pltpu.get_barrier_semaphore()
    for mate in mates:
        pl.semaphore_signal(barrier, inc=1, device_id={"rows": mate})
    for mate in (up, down):
        pl.semaphore_signal(barrier, inc=1, device_id={"snaps": mate})
    pl.semaphore_wait(barrier, n_bits + 2)

    def panel(k):
        return p_ref.at[:, k * n : (k + 1) * n]

    def relay(k, way):
        return pltpu.make_async_remote_copy(
            src_ref=panel(k),
            dst_ref=panel(k),
            send_sem=z_send.at[k, way],
            recv_sem=z_recv.at[k],
            device_id={"snaps": up if way else down},
        )

    def pass_on(k):
        @pl.when((snap >= k) & (snap < n_snaps - 1))
        def _():
            relay(k, 1).start()

        @pl.when((snap <= k) & (snap > 0))
        def _():
            relay(k, 0).start()

    for k in range(PANELS):

        @pl.when(snap == k)
        def _():
            own = pltpu.make_async_copy(w_ref.at[:, :n], panel(k), own_sem)
            own.start()
            own.wait()
            pass_on(k)

    order = list(range(PANELS - 1, -1, -1))

    def halves(k):
        width = v_refs[k].shape[1]
        split = (width // 256 + k // 2) * 128
        return ((0, split), (split, width - split))

    def spans(half):
        first, size, out = 0, n, []
        for b in bit_order(n_bits, half):
            size //= 2
            out.append((b, size, first + bits[b] * size, first + (1 - bits[b]) * size))
            first = first + bits[b] * size
        return out

    stages = [spans(0), spans(1)]

    def window(refs, k, half, first, size):
        low, width = halves(k)[half]
        return refs[k].at[pl.ds(pl.multiple_of(first, 8), size), low : low + width]

    def copy(k, half, step):
        down_step = step >= n_bits
        stage = 2 * n_bits - 1 - step if down_step else step
        b, size, kept, given = stages[half][stage]
        if down_step:
            src = dst = window(o_refs, k, half, kept, size)
        else:
            src = window(v_refs, k, half, given, size)
            dst = lands[(k * 2 + half) * n_bits + stage]
        return pltpu.make_async_remote_copy(
            src_ref=src,
            dst_ref=dst,
            send_sem=send_sems.at[k, half, step],
            recv_sem=recv_sems.at[k, half, step],
            device_id={"rows": mates[b]},
        )

    def finish(k, half, step):
        copy(k, half, step).wait_recv()
        if step < n_bits:
            b, size, kept, given = stages[half][step]
            view = window(v_refs, k, half, kept, size)
            into = view if step < n_bits - 1 else window(o_refs, k, half, kept, size)
            into[...] = view[...] + lands[(k * 2 + half) * n_bits + step][...]

    def compute(k):
        left = p_ref[:, k * n : (k + 1) * n]
        for i in range(k, PANELS):
            v_refs[k][:, (i - k) * n : (i - k + 1) * n] = dot6(
                left, p_ref[:, i * n : (i + 1) * n], ta=True
            )
        shift = (PANELS - k) * n
        for low in range(0, w_ref.shape[1], n):
            v_refs[k][:, shift + low : shift + low + n] = dot3(
                left, w_ref[:, low : low + n], ta=True
            )

    steps = 2 * n_bits
    for tick in range(steps + PANELS):
        for place, k in enumerate(order):
            step = tick - place
            if step == 0:

                @pl.when(snap != k)
                def _():
                    relay(k, 0).wait_recv()
                    pass_on(k)

                compute(k)
            for half in range(2):
                if 1 <= step <= steps:
                    finish(k, half, step - 1)
                if 0 <= step < steps:
                    copy(k, half, step).start()

    for k in range(PANELS):
        for half in range(2):
            for step in range(steps):
                copy(k, half, step).wait_send()

        @pl.when((snap >= k) & (snap < n_snaps - 1))
        def _():
            relay(k, 1).wait_send()

        @pl.when((snap <= k) & (snap > 0))
        def _():
            relay(k, 0).wait_send()


def reduced_by_copies(snapshots, n_rows, n_snaps):
    rows_dev, cols_dev = snapshots.shape
    n_bits = n_rows.bit_length() - 1
    widths = [(PANELS - k) * PANEL + cols_dev for k in range(PANELS)]
    lands = []
    for k, width in enumerate(widths):
        split = (width // 256 + k // 2) * 128
        for part in (split, width - split):
            lands += [pltpu.VMEM((PANEL >> (s + 1), part), F32) for s in range(n_bits)]
    vmem = pl.BlockSpec(memory_space=pltpu.VMEM)
    dma = pltpu.SemaphoreType.DMA
    return pl.pallas_call(
        functools.partial(reduce_kernel, n_rows, n_snaps),
        out_shape=[jax.ShapeDtypeStruct((rows_dev, PANELS * PANEL), F32)]
        + [jax.ShapeDtypeStruct((PANEL, width), F32) for width in widths],
        in_specs=[vmem],
        out_specs=[vmem] * (1 + PANELS),
        scratch_shapes=[pltpu.VMEM((PANEL, width), F32) for width in widths]
        + lands
        + [
            dma((PANELS, 2)),
            dma((PANELS,)),
            dma(()),
            dma((PANELS, 2, 2 * n_bits)),
            dma((PANELS, 2, 2 * n_bits)),
        ],
        compiler_params=pltpu.CompilerParams(
            collective_id=0, has_side_effects=True, vmem_limit_bytes=40 * 2**20
        ),
    )(snapshots)


def reduced_by_collectives(snapshots):
    total = PANEL * PANELS
    panels = lax.all_gather(snapshots[:, :PANEL], "snaps", axis=1, tiled=True)[:, :total]
    both = jnp.concatenate([panels, snapshots], axis=1)
    sums = lax.psum(
        [
            dot6(panels[:, k * PANEL : (k + 1) * PANEL], both[:, k * PANEL :], ta=True)
            for k in range(PANELS)
        ],
        "rows",
    )
    return [panels] + list(sums)


def shards(snapshots):
    rows_dev, cols_dev = snapshots.shape
    n_rows, n_snaps = lax.axis_size("rows"), lax.axis_size("snaps")
    root_rows = float(rows_dev * n_rows) ** 0.5
    total = PANEL * PANELS
    if n_rows & (n_rows - 1) == 0 and PANEL % (8 * n_rows) == 0:
        panels, *sums = reduced_by_copies(snapshots, n_rows, n_snaps)
    else:
        panels, *sums = reduced_by_collectives(snapshots)
    hbm = pl.BlockSpec(memory_space=pl.ANY)
    outs = [(rows_dev, cols_dev), (total, cols_dev)]
    operands = [panels, snapshots, *sums]
    buffers = [x.shape for x in operands] + outs
    buffers += [(rows_dev, total), (total, total), (total, cols_dev), (PANEL, PANEL), (PANEL, PANEL)]
    dma = pltpu.SemaphoreType.DMA
    return pl.pallas_call(
        functools.partial(factor_kernel, root_rows),
        out_shape=[jax.ShapeDtypeStruct(shape, F32) for shape in outs],
        in_specs=[hbm] * 5,
        out_specs=[hbm] * 2,
        scratch_shapes=[pltpu.VMEM(shape, F32) for shape in buffers]
        + [dma((6,)), dma((PANELS,)), dma((cols_dev // PANEL,))],
        compiler_params=pltpu.CompilerParams(vmem_limit_bytes=56 * 2**20),
    )(*operands)


def solution(mesh):
    assert mesh.shape["snaps"] >= PANELS
    return jax.shard_map(
        shards,
        mesh=mesh,
        in_specs=(P("rows", "snaps"),),
        out_specs=(P("rows", "snaps"), P(None, "snaps")),
        check_vma=False,
    )
```

```python
import functools

import jax
import jax.numpy as jnp
from jax import lax
from jax.experimental import pallas as pl
from jax.experimental.pallas import tpu as pltpu
from jax.sharding import PartitionSpec as P

PANEL = 384
PANELS = 3
PARTS = 4
F32 = jnp.float32
BF16 = jnp.bfloat16


def dims(ta, tb):
    return (((0 if ta else 1,), (1 if tb else 0,)), ((), ()))


def dot6(a, b, ta=False, tb=False):
    return lax.dot_general(
        a, b, dims(ta, tb), precision=lax.Precision.HIGHEST, preferred_element_type=F32
    )


def dot1(a, b, ta=False, tb=False):
    return lax.dot_general(
        a.astype(BF16), b.astype(BF16), dims(ta, tb), preferred_element_type=F32
    )


def dot3(a, b, ta=False, tb=False):
    a_hi, b_hi = a.astype(BF16), b.astype(BF16)
    a_lo = (a - a_hi.astype(F32)).astype(BF16)
    b_lo = (b - b_hi.astype(F32)).astype(BF16)
    d = dims(ta, tb)
    return (
        lax.dot_general(a_hi, b_lo, d, preferred_element_type=F32)
        + lax.dot_general(a_lo, b_hi, d, preferred_element_type=F32)
        + lax.dot_general(a_hi, b_hi, d, preferred_element_type=F32)
    )


def grid_ids(n):
    return (
        lax.broadcasted_iota(jnp.int32, (n, n), 0),
        lax.broadcasted_iota(jnp.int32, (n, n), 1),
    )


def direct_inverse(x_ref, a_ref):
    n = a_ref.shape[0]
    row_ids, col_ids = grid_ids(n)
    x_ref[...] = jnp.where(row_ids == col_ids, F32(1), F32(0))

    @pl.loop(0, n)
    def _(j):
        a = a_ref[...]
        a_row = jnp.sum(jnp.where(row_ids == j, a, F32(0)), axis=0, keepdims=True)
        x = x_ref[...]
        x_row = jnp.sum(jnp.where(row_ids == j, x, F32(0)), axis=0, keepdims=True)
        a_col = jnp.sum(jnp.where(col_ids == j, a, F32(0)), axis=1, keepdims=True)
        pivot = jnp.sum(jnp.where(col_ids[:1] == j, a_row, F32(0)), axis=1, keepdims=True)
        ratio = jnp.where(row_ids[:, :1] > j, a_col / pivot, F32(0))
        a_ref[...] = a - ratio * a_row
        x_ref[...] = jnp.where(row_ids == j, x / jnp.sqrt(pivot), x - ratio * x_row)


def newton_inverse(x_ref, a_ref):
    n = a_ref.shape[0]
    row_ids, col_ids = grid_ids(n)
    on_diag = row_ids == col_ids
    a = a_ref[...]
    diag = jnp.sum(jnp.where(on_diag, a, F32(0)), axis=1, keepdims=True)
    x_ref[...] = jnp.where(on_diag, lax.rsqrt(diag), F32(0))

    def step(dot, dot_half):
        x = x_ref[...]
        err = dot(dot(x, a_ref[...]), x, tb=True) - jnp.where(on_diag, F32(1), F32(0))
        half = jnp.where(row_ids > col_ids, err, jnp.where(on_diag, F32(0.5) * err, F32(0)))
        x_ref[...] = x - dot_half(half, x)
        return jnp.sum(err * err)

    def stage(state, dots, limit, count_limit):
        return lax.while_loop(
            lambda s: (s[0] < count_limit) & (s[1] > F32(limit)),
            lambda s: (s[0] + 1, step(*dots)),
            state,
        )

    count, size = stage((jnp.int32(0), F32(1e9)), (dot1, dot1), 0.3, 12)
    count, size = stage((count, F32(1e9)), (dot3, dot3), 1e-3, 20)
    count, size = stage((count, F32(1e9)), (dot6, dot3), 1e-6, 26)

    @pl.when(jnp.logical_not(size <= F32(1e-6)))
    def _():
        direct_inverse(x_ref, a_ref)


def factor_kernel(
    root_rows, p_hbm, w_hbm, v0_hbm, v1_hbm, v2_hbm, out_hbm, fac_hbm,
    p_ref, w_ref, v0_ref, v1_ref, v2_ref, out_ref, fac_ref,
    q_ref, u_ref, c_ref, t_ref, x_ref, in_sems, fac_sems, out_sems,
):
    v_refs = (v0_ref, v1_ref, v2_ref)
    snap = lax.axis_index("snaps")
    n = PANEL
    row_ids, col_ids = grid_ids(n)
    width = w_ref.shape[1]
    chunks = [(c, n) for c in range(0, width, n)]

    def blk(k):
        return slice(k * n, (k + 1) * n)

    loads = [
        pltpu.make_async_copy(v0_hbm.at[:, :n], v0_ref.at[:, :n], in_sems.at[0]),
        pltpu.make_async_copy(v0_hbm.at[:, n:], v0_ref.at[:, n:], in_sems.at[1]),
        pltpu.make_async_copy(p_hbm, p_ref, in_sems.at[2]),
        pltpu.make_async_copy(v1_hbm, v1_ref, in_sems.at[3]),
        pltpu.make_async_copy(v2_hbm, v2_ref, in_sems.at[4]),
        pltpu.make_async_copy(w_hbm, w_ref, in_sems.at[5]),
    ]
    for load in loads:
        load.start()
    loads[0].wait()
    stores = []

    for k in range(PANELS):
        acc = v_refs[k][:, :n]
        for j in range(k):
            acc = acc - dot6(u_ref[blk(j), blk(k)], u_ref[blk(j), blk(k)], ta=True)
        t_ref[...] = acc
        newton_inverse(x_ref, t_ref)
        if k == 0:
            for load in loads[1:]:
                load.wait()
        x = x_ref[...]
        for i in range(k + 1, PANELS):
            acc = v_refs[k][:, blk(i - k)]
            for j in range(k):
                acc = acc - dot3(u_ref[blk(j), blk(k)], u_ref[blk(j), blk(i)], ta=True)
            u_ref[blk(k), blk(i)] = dot3(x, acc)
        for low, size in chunks:
            cols = slice(low, low + size)
            shift = (PANELS - k) * n
            acc = v_refs[k][:, shift + low : shift + low + size]
            for j in range(k):
                acc = acc - dot3(u_ref[blk(j), blk(k)], c_ref[blk(j), cols], ta=True)
            coeffs = dot3(x, acc)
            if low == 0:
                keep = (snap > k) | ((snap == k) & (row_ids <= col_ids))
                coeffs = jnp.where(keep, coeffs, F32(0))
            c_ref[blk(k), cols] = coeffs
            fac_ref[blk(k), cols] = coeffs / root_rows
        stores.append(pltpu.make_async_copy(fac_ref.at[blk(k)], fac_hbm.at[blk(k)], fac_sems.at[k]))
        stores[-1].start()
        rest = p_ref[:, blk(k)]
        for j in range(k):
            rest = rest - dot3(q_ref[:, blk(j)], u_ref[blk(j), blk(k)])
        q_ref[:, blk(k)] = dot3(rest, x, tb=True)

    for at, (low, size) in enumerate(chunks):
        cols = slice(low, low + size)
        acc = w_ref[:, cols]
        for k in range(PANELS):
            acc = acc - dot3(q_ref[:, blk(k)], c_ref[blk(k), cols])
        if low == 0:
            for k in range(PANELS):
                acc = jnp.where(snap == k, q_ref[:, blk(k)] * root_rows, acc)
        out_ref[:, cols] = acc
        stores.append(pltpu.make_async_copy(out_ref.at[:, cols], out_hbm.at[:, cols], out_sems.at[at]))
        stores[-1].start()
    for store in stores:
        store.wait()


def part_spans(width, k):
    tiles = width // 128
    sizes = [tiles // PARTS] * PARTS
    for extra in range(tiles % PARTS):
        sizes[(extra + k // 2) % PARTS] += 1
    lows = [sum(sizes[:i]) for i in range(PARTS)]
    return [(low * 128, size * 128) for low, size in zip(lows, sizes)]


def bit_order(n_bits, half):
    return [0] + (list(range(1, n_bits)) if half % 2 == 0 else list(range(n_bits - 1, 0, -1)))


def reduce_kernel(n_rows, n_snaps, w_ref, p_ref, o0_ref, o1_ref, o2_ref, *scratch):
    v_refs, lands = scratch[:PANELS], scratch[PANELS:-5]
    z_send, z_recv, own_sem, send_sems, recv_sems = scratch[-5:]
    o_refs = (o0_ref, o1_ref, o2_ref)
    n = PANEL
    n_bits = n_rows.bit_length() - 1
    row = lax.axis_index("rows")
    snap = lax.axis_index("snaps")
    bits = [(row // 2**b) % 2 for b in range(n_bits)]
    mates = [row + (1 - 2 * bits[b]) * 2**b for b in range(n_bits)]
    up, down = lax.rem(snap + 1, n_snaps), lax.rem(snap + n_snaps - 1, n_snaps)

    barrier = pltpu.get_barrier_semaphore()
    for mate in mates:
        pl.semaphore_signal(barrier, inc=1, device_id={"rows": mate})
    for mate in (up, down):
        pl.semaphore_signal(barrier, inc=1, device_id={"snaps": mate})
    pl.semaphore_wait(barrier, n_bits + 2)

    def panel(k):
        return p_ref.at[:, k * n : (k + 1) * n]

    def relay(k, way):
        return pltpu.make_async_remote_copy(
            src_ref=panel(k),
            dst_ref=panel(k),
            send_sem=z_send.at[k, way],
            recv_sem=z_recv.at[k],
            device_id={"snaps": up if way else down},
        )

    def pass_on(k):
        @pl.when((snap >= k) & (snap < n_snaps - 1))
        def _():
            relay(k, 1).start()

        @pl.when((snap <= k) & (snap > 0))
        def _():
            relay(k, 0).start()

    for k in range(PANELS):

        @pl.when(snap == k)
        def _():
            own = pltpu.make_async_copy(w_ref.at[:, :n], panel(k), own_sem)
            own.start()
            own.wait()
            pass_on(k)

    order = list(range(PANELS - 1, -1, -1))

    def spans(half):
        first, size, out = 0, n, []
        for b in bit_order(n_bits, half):
            size //= 2
            out.append((b, size, first + bits[b] * size, first + (1 - bits[b]) * size))
            first = first + bits[b] * size
        return out

    stages = [spans(half) for half in range(PARTS)]

    def window(refs, k, half, first, size):
        low, width = part_spans(v_refs[k].shape[1], k)[half]
        return refs[k].at[pl.ds(pl.multiple_of(first, 8), size), low : low + width]

    def copy(k, half, step):
        down_step = step >= n_bits
        stage = 2 * n_bits - 1 - step if down_step else step
        b, size, kept, given = stages[half][stage]
        if down_step:
            src = dst = window(o_refs, k, half, kept, size)
        else:
            src = window(v_refs, k, half, given, size)
            dst = lands[(k * PARTS + half) * n_bits + stage]
        return pltpu.make_async_remote_copy(
            src_ref=src,
            dst_ref=dst,
            send_sem=send_sems.at[k, half, step],
            recv_sem=recv_sems.at[k, half, step],
            device_id={"rows": mates[b]},
        )

    def finish(k, half, step):
        copy(k, half, step).wait_recv()
        if step < n_bits:
            b, size, kept, given = stages[half][step]
            view = window(v_refs, k, half, kept, size)
            into = view if step < n_bits - 1 else window(o_refs, k, half, kept, size)
            into[...] = view[...] + lands[(k * PARTS + half) * n_bits + step][...]

    def compute(k):
        left = p_ref[:, k * n : (k + 1) * n]
        for i in range(k, PANELS):
            v_refs[k][:, (i - k) * n : (i - k + 1) * n] = dot6(
                left, p_ref[:, i * n : (i + 1) * n], ta=True
            )
        shift = (PANELS - k) * n
        for low in range(0, w_ref.shape[1], n):
            v_refs[k][:, shift + low : shift + low + n] = dot3(
                left, w_ref[:, low : low + n], ta=True
            )

    steps = 2 * n_bits
    for tick in range(steps + PANELS):
        for place, k in enumerate(order):
            step = tick - place
            if step == 0:

                @pl.when(snap != k)
                def _():
                    relay(k, 0).wait_recv()
                    pass_on(k)

                compute(k)
            for half in range(PARTS):
                if 1 <= step <= steps:
                    finish(k, half, step - 1)
                if 0 <= step < steps:
                    copy(k, half, step).start()

    for k in range(PANELS):
        for half in range(PARTS):
            for step in range(steps):
                copy(k, half, step).wait_send()

        @pl.when((snap >= k) & (snap < n_snaps - 1))
        def _():
            relay(k, 1).wait_send()

        @pl.when((snap <= k) & (snap > 0))
        def _():
            relay(k, 0).wait_send()


def reduced_by_copies(snapshots, n_rows, n_snaps):
    rows_dev, cols_dev = snapshots.shape
    n_bits = n_rows.bit_length() - 1
    widths = [(PANELS - k) * PANEL + cols_dev for k in range(PANELS)]
    lands = []
    for k, width in enumerate(widths):
        for _, part in part_spans(width, k):
            lands += [pltpu.VMEM((PANEL >> (s + 1), part), F32) for s in range(n_bits)]
    vmem = pl.BlockSpec(memory_space=pltpu.VMEM)
    dma = pltpu.SemaphoreType.DMA
    return pl.pallas_call(
        functools.partial(reduce_kernel, n_rows, n_snaps),
        out_shape=[jax.ShapeDtypeStruct((rows_dev, PANELS * PANEL), F32)]
        + [jax.ShapeDtypeStruct((PANEL, width), F32) for width in widths],
        in_specs=[vmem],
        out_specs=[vmem] * (1 + PANELS),
        scratch_shapes=[pltpu.VMEM((PANEL, width), F32) for width in widths]
        + lands
        + [
            dma((PANELS, 2)),
            dma((PANELS,)),
            dma(()),
            dma((PANELS, PARTS, 2 * n_bits)),
            dma((PANELS, PARTS, 2 * n_bits)),
        ],
        compiler_params=pltpu.CompilerParams(
            collective_id=0, has_side_effects=True, vmem_limit_bytes=40 * 2**20
        ),
    )(snapshots)


def reduced_by_collectives(snapshots):
    total = PANEL * PANELS
    panels = lax.all_gather(snapshots[:, :PANEL], "snaps", axis=1, tiled=True)[:, :total]
    both = jnp.concatenate([panels, snapshots], axis=1)
    sums = lax.psum(
        [
            dot6(panels[:, k * PANEL : (k + 1) * PANEL], both[:, k * PANEL :], ta=True)
            for k in range(PANELS)
        ],
        "rows",
    )
    return [panels] + list(sums)


def shards(snapshots):
    rows_dev, cols_dev = snapshots.shape
    n_rows, n_snaps = lax.axis_size("rows"), lax.axis_size("snaps")
    root_rows = float(rows_dev * n_rows) ** 0.5
    total = PANEL * PANELS
    if n_rows & (n_rows - 1) == 0 and PANEL % (8 * n_rows) == 0:
        panels, *sums = reduced_by_copies(snapshots, n_rows, n_snaps)
    else:
        panels, *sums = reduced_by_collectives(snapshots)
    hbm = pl.BlockSpec(memory_space=pl.ANY)
    outs = [(rows_dev, cols_dev), (total, cols_dev)]
    operands = [panels, snapshots, *sums]
    buffers = [x.shape for x in operands] + outs
    buffers += [(rows_dev, total), (total, total), (total, cols_dev), (PANEL, PANEL), (PANEL, PANEL)]
    dma = pltpu.SemaphoreType.DMA
    return pl.pallas_call(
        functools.partial(factor_kernel, root_rows),
        out_shape=[jax.ShapeDtypeStruct(shape, F32) for shape in outs],
        in_specs=[hbm] * 5,
        out_specs=[hbm] * 2,
        scratch_shapes=[pltpu.VMEM(shape, F32) for shape in buffers]
        + [dma((6,)), dma((PANELS,)), dma((cols_dev // PANEL,))],
        compiler_params=pltpu.CompilerParams(vmem_limit_bytes=40 * 2**20),
    )(*operands)


def solution(mesh):
    assert mesh.shape["snaps"] >= PANELS
    return jax.shard_map(
        shards,
        mesh=mesh,
        in_specs=(P("rows", "snaps"),),
        out_specs=(P("rows", "snaps"), P(None, "snaps")),
        check_vma=False,
    )
```
